32 devices in a mesh: rcv: 4 (over z), src: 8 (over y, x, core).
Axes of the slice: x: 2, y: 2, z: 4, core: 2. Of those that a mesh axis runs over, the one named last changes fastest.
Arguments:
- reflection: bfloat16 [2, 16384, 16384], P(None, 'rcv', 'src'), may hold values from -6 to 6
- green: bfloat16 [2, 16384, 512], P(None, 'rcv', 'src'), may hold values from -0.046875 to 0.046875
- tile_mask: int32 [64, 64], replicated, may hold values from 0 to 1, as said below
- reference_index: int32 [512], P(('rcv', 'src')), may hold values from 0 to 511
Outputs:
- aligned: float32 [512, 2, 512], P(('rcv', 'src'))
The draws below stay inside these ranges and needn't reach their ends.
Inputs may be any that keep to these rules, and one draw needn't show every extreme that they name: `tile_mask`: entries below the diagonal are 0.
All inputs are finite; a program needn't handle non-finite values.
Results may differ from the reference program's by a relative error of at most 0.02.
Values may be sent and summed in bfloat16 or wider, within the bound.
A program may use at most 256 MiB of HBM per device.

```python
import jax
import jax.numpy as jnp
from jax import lax

S = 16384
P_SIZE = 512
TILE = 256
TILES = 64
N_RCV = 4


def draw_tile_mask(key, part):
    levels = jax.random.randint(jax.random.fold_in(key, 17), (TILES, TILES), 0, 4)
    upper = jnp.arange(TILES)[:, None] <= jnp.arange(TILES)[None, :]
    return ((levels > 0) & upper).astype(jnp.int32)


def place_ends(result, stream_key, low, top_value):
    longest = result.shape.index(max(result.shape))
    spots = []
    for shift in (0, 1):
        where = [jax.random.randint(jax.random.fold_in(stream_key, axis), (), 0, length) for axis, length in enumerate(result.shape)]
        where[longest] = (where[longest] + shift) % result.shape[longest]
        spots.append(tuple(where))
    return result.at[spots[0]].set(low).at[spots[1]].set(top_value)


def block_levels(stream_key, extent, split, least, top_value):
    gain, own = 1.0, jax.random.fold_in(stream_key, 6)
    for dim, blocks in split:
        draws = jnp.exp(jax.random.uniform(jax.random.fold_in(own, dim), (blocks,), jnp.float32, least / len(split), top_value / len(split)))
        gain = gain * jnp.repeat(draws, extent[dim] // blocks).reshape([-1 if axis == dim else 1 for axis in range(len(extent))])
    return gain


def bell_draw(stream_key, shape, spread, reach, pieces=(), held_as=jnp.bfloat16):
    drawn = jax.random.normal(stream_key, shape, jnp.float32) * spread
    if len(pieces) > 0:
        drawn = block_levels(stream_key, shape, pieces, -0.22, 0.18) * drawn
    return jnp.clip(drawn, min=-reach, max=reach).astype(held_as)


def setup_inputs(seed: int = 0) -> dict:
    key_of = jax.random.split(jax.random.key(seed), 5)
    return {
        "reflection": bell_draw(key_of[0], (2, S, S), 1.0, 6.0, ((1, 4), (2, 8))),
        "green": bell_draw(key_of[1], (2, S, P_SIZE), S ** -0.5, 0.046875, ((1, 4), (2, 8))),
        "tile_mask": draw_tile_mask(jax.random.fold_in(key_of[4], 71), 0),
        "reference_index": place_ends(jax.random.randint(key_of[3], (P_SIZE,), 0, P_SIZE), jax.random.fold_in(key_of[3], 1), 0, P_SIZE - 1).astype(jnp.int32),
    }


exact_mode = lax.Precision.HIGHEST


def across(first, second):
    return lax.dot_general(first, second, (((0,), (0,)), ((), ())), preferred_element_type=jnp.float32)


def matmul(first, second):
    return jnp.dot(first, second, precision=exact_mode, preferred_element_type=jnp.float32)


def settle(value):
    return lax.optimization_barrier(value.astype(jnp.bfloat16)).astype(jnp.float32)


def reference(reflection, green, tile_mask, reference_index):
    block_rows = S // N_RCV
    tile_rows = block_rows // TILE
    col_tiles = jnp.arange(S // TILE)
    zero_value = jnp.zeros((), jnp.bfloat16)
    front_real = jnp.zeros((P_SIZE, S), jnp.float32)
    front_imag = jnp.zeros((P_SIZE, S), jnp.float32)
    back_real = jnp.zeros((P_SIZE, S), jnp.float32)
    back_imag = jnp.zeros((P_SIZE, S), jnp.float32)
    for block_index in range(N_RCV):
        row_start = block_index * block_rows
        measured = reflection[:, row_start:row_start + block_rows, :]
        tile_block = tile_mask[block_index * tile_rows:(block_index + 1) * tile_rows, :]
        row_tiles = block_index * tile_rows + jnp.arange(tile_rows)
        kept_tiles = tile_block == 1
        off_diag = kept_tiles & (row_tiles[:, None] != col_tiles[None, :])
        shaped = measured.reshape(2, tile_rows, TILE, S // TILE, TILE)
        acquired = jnp.where(kept_tiles[None, :, None, :, None], shaped, zero_value).reshape(2, block_rows, S)
        mirror_part = jnp.where(off_diag[None, :, None, :, None], shaped, zero_value).reshape(2, block_rows, S)
        green_real = green[0, row_start:row_start + block_rows, :]
        green_imag = green[1, row_start:row_start + block_rows, :]
        front_real = front_real + settle(across(green_real, acquired[0]) + across(green_imag, acquired[1]))
        front_imag = front_imag + settle(across(green_real, acquired[1]) - across(green_imag, acquired[0]))
        back_real = back_real + settle(across(green_real, mirror_part[0]) - across(green_imag, mirror_part[1]))
        back_imag = back_imag + settle(across(green_real, mirror_part[1]) + across(green_imag, mirror_part[0]))
    full_real = green[0].astype(jnp.float32)
    full_imag = green[1].astype(jnp.float32)
    focal_real = matmul(front_real, full_real) - matmul(front_imag, full_imag)
    focal_real = focal_real + (matmul(back_real, full_real) + matmul(back_imag, full_imag)).T
    focal_imag = matmul(front_real, full_imag) + matmul(front_imag, full_real)
    focal_imag = focal_imag + (matmul(back_imag, full_real) - matmul(back_real, full_imag)).T
    chosen = jnp.arange(P_SIZE).astype(jnp.int32)[None, :] == reference_index.astype(jnp.int32)[:, None]
    anchor_real = jnp.sum(jnp.where(chosen, focal_real, 0.0), axis=1)[:, None]
    anchor_imag = jnp.sum(jnp.where(chosen, focal_imag, 0.0), axis=1)[:, None]
    out_real = focal_real * anchor_real + focal_imag * anchor_imag
    out_imag = focal_imag * anchor_real - focal_real * anchor_imag
    return jnp.stack([out_real, out_imag], axis=1)
```

```python
import functools

import jax
import jax.numpy as jnp
from jax import lax
from jax.experimental import pallas as pl
from jax.experimental.pallas import tpu as pltpu
from jax.sharding import PartitionSpec as P

MESH = pl.DeviceIdType.MESH
TILE = 256
f32 = jnp.float32
bf16 = jnp.bfloat16


def dot_nn(a, b):
    return lax.dot_general(a, b, (((1,), (0,)), ((), ())), preferred_element_type=f32)


def dot_nt(a, b):
    return lax.dot_general(a, b, (((1,), (1,)), ((), ())), preferred_element_type=f32)


def kernel(
    n_rcv, n_src, mask_ref, piece_ref, refl_ref, focal_ref,
    gr, gc, y, abuf, acc, quad, slab, arrived,
    gr_send, fw_send, gr_recv, gc_send, gc_recv, gc_local, own_sem, load_sem, slab_send, slab_recv,
):
    n_dev = n_rcv * n_src
    r = lax.axis_index("rcv")
    s = lax.axis_index("src")
    me = r * n_src + s
    partner = s + 1 - 2 * lax.rem(s, 2)
    n_p, rows = gr.shape[1], gr.shape[2]
    cols = gc.shape[2]
    own_p = n_p // n_src
    out_rows = n_p // n_dev
    n_tiles = cols // TILE
    row_tiles = rows // TILE

    def last_col(src):
        return (src + 1) * cols

    def is_active(rcv, src):
        return rcv * rows < last_col(src)

    def pair_active(rcv, src):
        return rcv * rows < last_col(src - lax.rem(src, 2) + 1)

    active = is_active(r, s)
    gathers = pair_active(r, s)
    holder = (s * cols) // rows
    offset = pl.multiple_of(s * cols - holder * rows, TILE)
    on_diag = r == holder

    def load(t):
        slot = lax.rem(t, 2)
        return pltpu.make_async_copy(
            refl_ref.at[:, :, pl.ds(pl.multiple_of(t * TILE, TILE), TILE)],
            abuf.at[slot],
            load_sem.at[slot],
        )

    def gr_slot(i):
        return gr.at[:, pl.ds(pl.multiple_of(i * own_p, own_p), own_p), :]

    def gc_slot(i):
        return gc.at[:, pl.ds(pl.multiple_of(i * own_p, own_p), own_p), :]

    own_copy = pltpu.make_async_copy(piece_ref, gr_slot(s), own_sem)

    @pl.when(active)
    def _():
        load(0).start()

    @pl.when(gathers)
    def _():
        own_copy.start()

    barrier = pltpu.get_barrier_semaphore()

    @pl.loop(1, n_dev)
    def _(i):
        other = lax.rem(me + i, n_dev)
        pl.semaphore_signal(
            barrier, inc=1, device_id=(other // n_src, lax.rem(other, n_src)), device_id_type=MESH
        )

    pl.semaphore_wait(barrier, n_dev - 1)

    def piece_to(dest):
        return pltpu.make_async_remote_copy(
            src_ref=piece_ref, dst_ref=gr_slot(s), send_sem=gr_send.at[dest], recv_sem=gr_recv.at[s],
            device_id=(r, dest), device_id_type=MESH,
        )

    def forward(i):
        return pltpu.make_async_remote_copy(
            src_ref=gr_slot(i), dst_ref=gr_slot(i), send_sem=fw_send.at[i], recv_sem=gr_recv.at[i],
            device_id=(r, partner), device_id_type=MESH,
        )

    def upward(i):
        return lax.rem(i // 2, 2) == 1

    def source_target(i):
        return jnp.where(upward(i), 0, r - 1)

    def from_source(i):
        return pltpu.make_async_remote_copy(
            src_ref=gr.at[:, pl.ds(pl.multiple_of(i * own_p, own_p), own_p), pl.ds(offset, cols)],
            dst_ref=gc_slot(i), send_sem=gc_send.at[i], recv_sem=gc_recv.at[i],
            device_id=(source_target(i), s), device_id_type=MESH,
        )

    def to_local(i):
        return pltpu.make_async_copy(
            gr.at[:, pl.ds(pl.multiple_of(i * own_p, own_p), own_p), pl.ds(offset, cols)],
            gc_slot(i), gc_local.at[i],
        )

    def relay(i):
        return pltpu.make_async_remote_copy(
            src_ref=gc_slot(i), dst_ref=gc_slot(i), send_sem=gc_send.at[i], recv_sem=gc_recv.at[i],
            device_id=(jnp.where(upward(i), r + 1, r - 1), s), device_id_type=MESH,
        )

    def relays(i):
        return (jnp.logical_not(upward(i)) & (r >= 1)) | (upward(i) & (r + 1 < holder))

    def share(i):
        @pl.when(on_diag)
        def _():
            to_local(i).start()

            @pl.when(r >= 1)
            def _():
                from_source(i).start()

    same = [lax.rem(s + 2 * i, n_src) for i in range(1, n_src // 2)]
    for dest in same:
        @pl.when(pair_active(r, dest))
        def _():
            piece_to(dest).start()

    @pl.when(gathers)
    def _():
        piece_to(partner).start()
        own_copy.wait()
        share(s)
        forward(partner).wait_recv()
        share(partner)
        for i in same:
            forward(i).wait_recv()
            forward(i).start()
            share(i)
        for i in same:
            twin = i + 1 - 2 * lax.rem(i, 2)
            forward(twin).wait_recv()
            share(twin)

    per = -(-n_src // n_tiles)
    step_rows = min(rows, 1024)

    @pl.when(active)
    def _():
        @pl.loop(0, n_tiles)
        def _(t):
            slot = lax.rem(t, 2)
            load(t).wait()

            @pl.when(t + 1 < n_tiles)
            def _():
                load(t + 1).start()

            for i in range(per):
                p = t * per + i

                @pl.when((p < n_src) & jnp.logical_not(on_diag))
                def _():
                    relay(p).wait_recv()

                    @pl.when(relays(p))
                    def _():
                        relay(p).start()

            col_end = s * cols + (t + 1) * TILE
            for k in range(rows // step_rows):
                def step():
                    for j in range(step_rows // TILE):
                        m = mask_ref[k * (step_rows // TILE) + j, t]
                        at = pl.ds(k * step_rows + j * TILE, TILE)
                        for z in range(2):
                            tile = abuf[slot, z, at, :]
                            abuf[slot, z, at, :] = jnp.where(m == 1, tile, jnp.zeros_like(tile))
                    left = gr[:, :, k * step_rows:(k + 1) * step_rows].reshape(2 * n_p, step_rows)
                    for z in range(2):
                        term = dot_nn(left, abuf[slot, z, k * step_rows:(k + 1) * step_rows, :])
                        if k == 0:
                            acc[z] = term
                        else:
                            acc[z] += term

                if k == 0:
                    step()
                else:
                    pl.when(r * rows + k * step_rows < col_end)(step)
            at = pl.ds(pl.multiple_of(t * TILE, TILE), TILE)
            for z in range(2):
                y[z, :, at] = acc[z].astype(bf16)

        @pl.when(on_diag)
        def _():
            @pl.loop(0, n_src)
            def _(i):
                to_local(i).wait()

        def second(direct):
            @pl.loop(0, n_p // TILE)
            def _(b):
                at = pl.ds(pl.multiple_of(b * TILE, TILE), TILE)
                g_re = gc[0, at, :]
                g_im = gc[1, at, :]
                s_re = dot_nt(y[0, :n_p, :], g_re) + dot_nt(y[0, n_p:, :], g_im)
                k_im = dot_nt(y[1, :n_p, :], g_im) - dot_nt(y[1, n_p:, :], g_re)
                if direct:
                    quad[0, :, at] = s_re - k_im
                quad[2, :, at] = s_re + k_im
                s_im = dot_nt(y[1, :n_p, :], g_re) + dot_nt(y[1, n_p:, :], g_im)
                k_re = dot_nt(y[0, :n_p, :], g_im) - dot_nt(y[0, n_p:, :], g_re)
                if direct:
                    quad[1, :, at] = s_im + k_re
                quad[3, :, at] = s_im - k_re

        second(True)

        first_tile = s * n_tiles - r * row_tiles
        overlaps = (first_tile < row_tiles) & (first_tile + n_tiles > 0)

        @pl.when(overlaps)
        def _():
            @pl.loop(0, n_tiles)
            def _(t):
                row = first_tile + t

                @pl.when((row >= 0) & (row < row_tiles))
                def _():
                    at_r = pl.ds(pl.multiple_of(row * TILE, TILE), TILE)
                    at_c = pl.ds(pl.multiple_of(t * TILE, TILE), TILE)
                    tile_copy = pltpu.make_async_copy(
                        refl_ref.at[:, at_r, at_c], abuf.at[0, :, pl.ds(0, TILE), :], own_sem
                    )
                    tile_copy.start()
                    tile_copy.wait()
                    m = mask_ref[row, t]
                    left = gr[:, :, at_r].reshape(2 * n_p, TILE)
                    for z in range(2):
                        tile = abuf[0, z, :TILE, :]
                        tile = jnp.where(m == 1, tile, jnp.zeros_like(tile))
                        kept = y[z, :, at_c].astype(f32) - dot_nn(left, tile)
                        y[z, :, at_c] = kept.astype(bf16)

            second(False)

        for part in range(2):
            for b in range(n_p // TILE):
                turned = quad[2 + part, :, b * TILE:(b + 1) * TILE].T
                quad[part, b * TILE:(b + 1) * TILE, :] += turned

        group = max(16, out_rows)

        @pl.loop(0, n_p // group)
        def _(g):
            at = pl.ds(pl.multiple_of(g * group, group), group)
            for part in range(2):
                block = quad[part, at, :]
                for j in range(group // out_rows):
                    slab[g * (group // out_rows) + j, :, part * n_p:(part + 1) * n_p] = block[
                        j * out_rows:(j + 1) * out_rows
                    ].astype(bf16)

    def slab_to(other):
        return pltpu.make_async_remote_copy(
            src_ref=slab.at[other], dst_ref=arrived.at[me], send_sem=slab_send.at[other],
            recv_sem=slab_recv.at[me],
            device_id=(other // n_src, lax.rem(other, n_src)), device_id_type=MESH,
        )

    def slab_from(other):
        return pltpu.make_async_remote_copy(
            src_ref=slab.at[me], dst_ref=arrived.at[other], send_sem=slab_send.at[other],
            recv_sem=slab_recv.at[other],
            device_id=(other // n_src, lax.rem(other, n_src)), device_id_type=MESH,
        )

    @pl.when(active)
    def _():
        @pl.loop(1, n_dev)
        def _(i):
            slab_to(lax.rem(me + i, n_dev)).start()

    focal_ref[...] = jnp.zeros_like(focal_ref)

    @pl.when(active)
    def _():
        focal_ref[...] = slab[me].astype(f32)

    for other in range(n_dev):
        if (other // n_src) * rows < (other % n_src + 1) * cols:
            @pl.when(me != other)
            def _():
                slab_from(other).wait_recv()
                focal_ref[...] += arrived[other].astype(f32)

    @pl.when(active)
    def _():
        @pl.loop(1, n_dev)
        def _(i):
            slab_to(lax.rem(me + i, n_dev)).wait_send()

    for dest in same:
        @pl.when(pair_active(r, dest))
        def _():
            piece_to(dest).wait_send()

    @pl.when(gathers)
    def _():
        piece_to(partner).wait_send()
        for i in same:
            forward(i).wait_send()

        @pl.loop(0, n_src)
        def _(i):
            @pl.when(on_diag & (r >= 1))
            def _():
                from_source(i).wait_send()

            @pl.when(active & jnp.logical_not(on_diag) & relays(i))
            def _():
                relay(i).wait_send()


def body(reflection, green, tile_mask, reference_index):
    rows, cols = reflection.shape[1], reflection.shape[2]
    n_rcv, n_src = lax.axis_size("rcv"), lax.axis_size("src")
    n_dev = n_rcv * n_src
    own_p = green.shape[2]
    n_p = own_p * n_src
    out_rows = n_p // n_dev
    r, s = lax.axis_index("rcv"), lax.axis_index("src")
    row_tiles, n_tiles = rows // TILE, cols // TILE
    tile_block = lax.dynamic_slice(tile_mask, (r * row_tiles, s * n_tiles), (row_tiles, n_tiles))
    piece = jnp.swapaxes(green, 1, 2)
    dma = pltpu.SemaphoreType.DMA
    any_spec = pl.BlockSpec(memory_space=pl.ANY)
    focal = pl.pallas_call(
        functools.partial(kernel, n_rcv, n_src),
        out_shape=jax.ShapeDtypeStruct((out_rows, 2 * n_p), f32),
        in_specs=[pl.BlockSpec(memory_space=pltpu.SMEM), any_spec, any_spec],
        out_specs=pl.BlockSpec(memory_space=pltpu.VMEM),
        scratch_shapes=[
            pltpu.VMEM((2, n_p, rows), bf16),
            pltpu.VMEM((2, n_p, cols), bf16),
            pltpu.VMEM((2, 2 * n_p, cols), bf16),
            pltpu.VMEM((2, 2, rows, TILE), bf16),
            pltpu.VMEM((2, 2 * n_p, TILE), f32),
            pltpu.VMEM((4, n_p, n_p), f32),
            pltpu.VMEM((n_dev, out_rows, 2 * n_p), bf16),
            pltpu.VMEM((n_dev, out_rows, 2 * n_p), bf16),
            dma((n_src,)), dma((n_src,)), dma((n_src,)), dma((n_src,)), dma((n_src,)), dma((n_src,)),
            dma, dma((2,)), dma((n_dev,)), dma((n_dev,)),
        ],
        compiler_params=pltpu.CompilerParams(
            collective_id=0, has_side_effects=True, vmem_limit_bytes=60 * 1024 * 1024
        ),
        name="focus",
    )(tile_block, piece, reflection)
    focal_real = focal[:, :n_p]
    focal_imag = focal[:, n_p:]
    chosen = jnp.arange(n_p)[None, :] == reference_index[:, None]
    anchor_real = jnp.sum(jnp.where(chosen, focal_real, 0.0), axis=1)[:, None]
    anchor_imag = jnp.sum(jnp.where(chosen, focal_imag, 0.0), axis=1)[:, None]
    out_real = focal_real * anchor_real + focal_imag * anchor_imag
    out_imag = focal_imag * anchor_real - focal_real * anchor_imag
    return jnp.stack([out_real, out_imag], axis=1)


def solution(mesh):
    return jax.shard_map(
        body,
        mesh=mesh,
        in_specs=(P(None, "rcv", "src"), P(None, "rcv", "src"), P(), P(("rcv", "src"))),
        out_specs=P(("rcv", "src"), None, None),
        check_vma=False,
    )
```
